128 devices in a mesh: slab: 8 (over y, z_lo), row: 4 (over z_hi, core), col: 4 (over x).
Axes of the slice: x: 4, y: 4, z: 4 (z_hi: 2, z_lo: 2; z = z_hi * 2 + z_lo), core: 2. Of those that a mesh axis runs over, the one named last changes fastest.
Arguments:
- inverse: bfloat16 [8, 8192, 4, 2048], P('slab', 'row', None, 'col'), may hold values from -0.0625 to 0.0625
- sources: bfloat16 [8, 4, 8192, 128], P('slab', None, ('row', 'col')), may hold values from -6 to 6
- coupling: float32 [8, 2, 8192], P('slab', None, ('row', 'col')), may hold values from -1 to 1
- plan: int32 [6, 8, 2], replicated, may hold values from 0 to 3
Outputs:
- up_out: bfloat16 [8, 8192, 128], P('slab', ('row', 'col'))
- down_out: bfloat16 [8, 8192, 128], P('slab', ('row', 'col'))
The draws below stay inside these ranges and needn't reach their ends.
Inputs may be any that keep to these rules, and one draw needn't show every extreme that they name: `plan`: each entry names one of the 4 stored batches of its slab.
All inputs are finite; a program needn't handle non-finite values.
Results may differ from the reference program's by a relative error of at most 0.023.
Values may be sent and summed in bfloat16 or wider, within the bound.
No kernel may reach another device: no remote copies, remote signals or barrier semaphores. Data moves between devices by JAX's collectives and lax.ppermute only.
A program may use at most 64 MiB of HBM per device.

```python
import jax
import jax.numpy as jnp
from jax import lax

M = 8192
B = 128
TICKS = 6
NBATCH = 4
SLABS = 8
N_ROW = 4
N_COL = 4


def draw_coupling(key, part):
    base = jax.random.fold_in(key, 7331)
    sign_key, size_key = jax.random.split(base)
    sign_bits = jax.random.randint(sign_key, (SLABS, 2, M), 0, 2)
    signs = sign_bits.astype(jnp.float32) * 2.0 - 1.0
    lower = 0.9
    magnitude = jax.random.uniform(size_key, (SLABS, 2, M), jnp.float32, lower, 1.0)
    return (signs * magnitude).astype(jnp.float32)


def plant(values, rng, least, largest):
    extent = values.shape
    index_at = [jax.random.randint(jax.random.fold_in(rng, axis), (), 0, extent[axis]) for axis in range(len(extent))]
    values = values.at[tuple(index_at)].set(least)
    longest = extent.index(max(extent))
    index_at[longest] = (index_at[longest] + 1) % extent[longest]
    return values.at[tuple(index_at)].set(largest)


def shard_levels(stream_key, dims, pieces, least, top_value):
    loudness, own = 1.0, jax.random.fold_in(stream_key, 6)
    for position, parts in pieces:
        steps = jnp.exp(jax.random.uniform(jax.random.fold_in(own, position), (parts,), jnp.float32, least / len(pieces), top_value / len(pieces)))
        loudness = loudness * jnp.repeat(steps, dims[position] // parts).reshape([-1 if axis == position else 1 for axis in range(len(dims))])
    return loudness


def noise(rng, extent, width, bound, shards=(), kind=jnp.bfloat16):
    factor_of = shard_levels(rng, extent, shards, -0.22, 0.18) if shards else 1.0
    values = jax.random.normal(rng, extent, jnp.float32) * width * factor_of
    return jnp.minimum(jnp.maximum(values, -bound), bound).astype(kind)


def setup_inputs(seed: int = 0) -> dict:
    streams_of = jax.random.split(jax.random.key(seed), 5)
    inverse = noise(streams_of[0], (SLABS, M, N_ROW, M // N_ROW), M ** -0.5, 0.0625, ((0, 8), (1, 4), (3, 4)))
    sources = noise(streams_of[1], (SLABS, NBATCH, M, B), 1.0, 6.0, ((0, 8), (2, 16)))
    coupling = draw_coupling(jax.random.fold_in(streams_of[4], 71), 0)
    plan = plant(jax.random.randint(streams_of[3], (TICKS, SLABS, 2), 0, NBATCH), jax.random.fold_in(streams_of[3], 1), 0, NBATCH - 1).astype(jnp.int32)
    return dict(inverse=inverse, sources=sources, coupling=coupling, plan=plan)


def apply_up(matrix, vector):
    piece_rows = M // (N_ROW * N_COL)
    matrix_split = matrix.reshape(M, N_ROW, N_COL, piece_rows)
    vector_split = vector.reshape(N_ROW, N_COL, piece_rows, B)
    running = jnp.zeros((M, B), jnp.float32)
    for column_group in range(N_COL):
        columns = matrix_split[:, :, column_group, :].reshape(M, N_ROW * piece_rows)
        chosen = vector_split[:, column_group].reshape(N_ROW * piece_rows, B)
        partial_value = jnp.dot(columns, chosen, preferred_element_type=jnp.float32)
        rounded = lax.optimization_barrier(partial_value.astype(jnp.bfloat16))
        running = running + rounded.astype(jnp.float32)
    return running.astype(jnp.bfloat16)


def apply_down(matrix, vector):
    row_count = M // N_ROW
    running = jnp.zeros((M, B), jnp.float32)
    for row_group in range(N_ROW):
        row_block = matrix[row_group * row_count:(row_group + 1) * row_count]
        chosen = vector[row_group * row_count:(row_group + 1) * row_count]
        partial_value = lax.dot_general(row_block, chosen, (((0,), (0,)), ((), ())), preferred_element_type=jnp.float32)
        rounded = lax.optimization_barrier(partial_value.astype(jnp.bfloat16))
        running = running + rounded.astype(jnp.float32)
    return running.astype(jnp.bfloat16)


def reference(inverse, sources, coupling, plan):
    full = inverse.reshape(SLABS, M, M)
    up_out = jnp.zeros((SLABS, M, B), jnp.bfloat16)
    down_out = jnp.zeros((SLABS, M, B), jnp.bfloat16)
    slab_numbers = jnp.arange(SLABS, dtype=jnp.int32)
    zero_slab = jnp.zeros((1, M, B), jnp.bfloat16)
    for tick_index in range(TICKS):
        up_prev = jnp.concatenate([zero_slab, up_out[:-1]], axis=0)
        down_prev = jnp.concatenate([down_out[1:], zero_slab], axis=0)
        up_source = sources[slab_numbers, plan[tick_index, :, 0]]
        down_source = sources[slab_numbers, plan[tick_index, :, 1]]
        up_in = (up_source.astype(jnp.float32) + coupling[:, 0, :, None] * up_prev.astype(jnp.float32)).astype(jnp.bfloat16)
        down_in = (down_source.astype(jnp.float32) + coupling[:, 1, :, None] * down_prev.astype(jnp.float32)).astype(jnp.bfloat16)
        new_up = []
        new_down = []
        for slab_number in range(SLABS):
            new_up.append(apply_up(full[slab_number], up_in[slab_number]))
            new_down.append(apply_down(full[slab_number], down_in[slab_number]))
        up_out = jnp.stack(new_up)
        down_out = jnp.stack(new_down)
    return up_out, down_out
```

```python
import jax
import jax.numpy as jnp
from jax import lax
from jax.experimental import pallas as pl
from jax.experimental.pallas import tpu as pltpu
from jax.sharding import PartitionSpec as P

TICKS = 6

VMEM = pl.BlockSpec(memory_space=pltpu.VMEM)
SMEM = pl.BlockSpec(memory_space=pltpu.SMEM)


def f32dot(a, b):
    return jnp.dot(a, b, preferred_element_type=jnp.float32)


def up_first_kernel(idx, blocks, x0, x1, acc):
    @pl.when(idx[8] > 0)
    def _():
        for m in range(4):
            acc[m] = f32dot(blocks[idx[m], idx[4]], x0[...]) + f32dot(blocks[idx[m], idx[5]], x1[...])


def up_last_kernel(m, idx, blocks, x2, x3, acc, out):
    @pl.when(idx[8] > 0)
    def _():
        total = acc[m] + f32dot(blocks[idx[m], idx[6]], x2[...]) + f32dot(blocks[idx[m], idx[7]], x3[...])
        out[...] = total.astype(out.dtype)

    @pl.when(idx[8] == 0)
    def _():
        out[...] = jnp.zeros(out.shape, out.dtype)


def down_first_kernel(idx, blocks, x0, acc):
    @pl.when(idx[9] > 0)
    def _():
        for j in range(4):
            acc[j] = f32dot(x0[...], blocks[idx[0], idx[4 + j]])


def down_last_kernel(idx, blocks, x1, x2, x3, acc, kept, sent):
    def total(j):
        return (
            acc[j]
            + f32dot(x1[...], blocks[idx[1], idx[4 + j]])
            + f32dot(x3[...], blocks[idx[3], idx[4 + j]])
            + f32dot(x2[...], blocks[idx[2], idx[4 + j]])
        )

    @pl.when(idx[9] > 0)
    def _():
        sent[0] = total(1).astype(sent.dtype)
        sent[1] = total(3).astype(sent.dtype)
        kept[0] = total(0)
        kept[1] = total(2)

    @pl.when(idx[9] == 0)
    def _():
        sent[...] = jnp.zeros(sent.shape, sent.dtype)
        kept[...] = jnp.zeros(kept.shape, kept.dtype)


def call(kernel, outs, name):
    def run(*args):
        return pl.pallas_call(
            kernel,
            out_shape=outs,
            in_specs=[SMEM] + [VMEM] * (len(args) - 1),
            out_specs=jax.tree.map(lambda _: VMEM, outs),
            compiler_params=pltpu.CompilerParams(vmem_limit_bytes=24 << 20),
            name=name,
        )(*args)

    return run


def wide(value):
    return value.astype(jnp.float32)


def narrow(value):
    return value.astype(jnp.bfloat16)


def per_device(inverse, sources, coupling, plan):
    slabs = lax.axis_size("slab")
    rows = lax.axis_size("row")
    cols = lax.axis_size("col")
    slab = lax.axis_index("slab")
    row = lax.axis_index("row")
    col = lax.axis_index("col")
    piece = sources.shape[2]
    width = sources.shape[3]
    top = slabs - 1
    idx_base = jnp.concatenate(
        [(col + jnp.arange(cols)) % cols, row ^ jnp.arange(rows)]
    ).astype(jnp.int32)

    def at_slabs(pairs, names=("slab", "row")):
        return pairs

    def over_row(value, active, flip):
        pairs = [(s * rows + r, s * rows + (r ^ flip)) for s in active for r in range(rows)]
        return lax.ppermute(value, ("slab", "row"), pairs)

    def over_slab(value, active, step, flip):
        pairs = [
            (s * rows + r, ((s + step) % slabs) * rows + (r ^ flip)) for s in active for r in range(rows)
        ]
        return lax.ppermute(value, ("slab", "row"), pairs)

    def over_col(value, active, step):
        pairs = [(s * cols + c, s * cols + (c + step) % cols) for s in active for c in range(cols)]
        return lax.ppermute(value, ("slab", "col"), pairs)

    blocks = inverse[0].reshape(cols, piece, rows, piece).transpose(0, 2, 1, 3)
    stored = sources[0]
    up_gain = coupling[0, 0][:, None]
    down_gain = coupling[0, 1][None, :]
    stored_t = jnp.swapaxes(stored, 1, 2)
    everyone = list(range(slabs))
    next_stored = over_slab(stored, everyone, -1, 0)
    next_gain = over_slab(coupling[0, 0], everyone, -1, 0)[:, None]
    next_slab = (slab + 1) % slabs

    def pick(values, tick, which, at):
        return lax.dynamic_index_in_dim(values, plan[tick, at, which], 0, keepdims=False)

    acc_up = jax.ShapeDtypeStruct((cols, piece, width), jnp.float32)
    acc_down = jax.ShapeDtypeStruct((rows, width, piece), jnp.float32)
    up_out = None
    down_in = None
    for tick in range(TICKS):
        last = tick == TICKS - 1
        up_on = [s for s in range(slabs) if s <= tick + slabs - TICKS]
        down_on = [s for s in range(slabs) if s >= TICKS - 1 - tick]
        flags = jnp.stack([slab <= up_on[-1], slab >= down_on[0]]).astype(jnp.int32)
        idx = jnp.concatenate([idx_base, flags])

        if tick == 0:
            down_in = pick(stored_t, 0, 1, slab)
        d1 = over_col(down_in, down_on, -1)
        d2 = over_col(down_in, down_on, -2)
        d3 = over_col(down_in, down_on, -3)
        if tick == 0:
            u0 = pick(stored, 0, 0, slab)
            u2 = over_row(u0, up_on, 2)
        else:
            carried = jnp.where(slab == top, 0.0, wide(up_out))
            up_in = narrow(wide(pick(next_stored, tick, 0, next_slab)) + next_gain * carried)
            senders = [(s - 1) % slabs for s in up_on]
            u0 = over_slab(up_in, senders, 1, 0)
            u2 = over_slab(up_in, senders, 1, 2)
        u1 = over_row(u0, up_on, 1)
        u3 = over_row(u2, up_on, 1)

        acc = call(up_first_kernel, acc_up, "up_first")(idx, blocks, u0, u1)
        parts = []
        for m in (2, 1, 3, 0):
            kind = jax.ShapeDtypeStruct((piece, width), jnp.bfloat16 if m else jnp.float32)
            part = call(lambda *refs, m=m: up_last_kernel(m, *refs), kind, f"up_last_{m}")(idx, blocks, u2, u3, acc)
            parts.append(over_col(part, up_on, m) if m else part)
        up_out = narrow(parts[3] + wide(parts[0]) + wide(parts[1]) + wide(parts[2]))

        acc = call(down_first_kernel, acc_down, "down_first")(idx, blocks, down_in)
        kept, sent = call(
            down_last_kernel,
            (
                jax.ShapeDtypeStruct((2, width, piece), jnp.float32),
                jax.ShapeDtypeStruct((2, width, piece), jnp.bfloat16),
            ),
            "down_last",
        )(idx, blocks, d1, d2, d3, acc)
        got = over_row(sent, down_on, 1)
        if last:
            got2 = over_row(narrow(kept[1] + wide(got[1])), down_on, 2)
            down_out = narrow(kept[0] + wide(got[0]) + wide(got2))
        else:
            movers = [s for s in down_on if s > 0]
            same = over_slab(narrow(kept[0] + wide(got[0])), movers, -1, 0)
            cross = over_slab(narrow(kept[1] + wide(got[1])), movers, -1, 2)
            down_recv = narrow(wide(same) + wide(cross))
            down_in = narrow(wide(pick(stored_t, tick + 1, 1, slab)) + down_gain * wide(down_recv))
    return (up_out[None], jnp.swapaxes(down_out, 0, 1)[None])


def solution(mesh):
    placed = (
        P("slab", "row", None, "col"),
        P("slab", None, ("row", "col"), None),
        P("slab", None, ("row", "col")),
        P(),
    )
    return jax.shard_map(
        per_device,
        mesh=mesh,
        in_specs=placed,
        out_specs=(P("slab", ("row", "col"), None), P("slab", ("row", "col"), None)),
        check_vma=False,
    )
```

```python
import jax
import jax.numpy as jnp
from jax import lax
from jax.experimental import pallas as pl
from jax.experimental.pallas import tpu as pltpu
from jax.sharding import PartitionSpec as P

TICKS = 6
GROUPED = (7, 7, 7, 7, 7, 7)

VMEM = pl.BlockSpec(memory_space=pltpu.VMEM)
SMEM = pl.BlockSpec(memory_space=pltpu.SMEM)
ANY = pl.BlockSpec(memory_space=pl.ANY)


def f32dot(a, b):
    return jnp.dot(a, b, preferred_element_type=jnp.float32)


def wide(value):
    return value.astype(jnp.float32)


def narrow(value):
    return value.astype(jnp.bfloat16)


def shape(*lengths, kind=jnp.bfloat16):
    return jax.ShapeDtypeStruct(lengths, kind)


def call(kernel, outs, *args, specs=None, scratch=(), limit=24 << 20):
    return pl.pallas_call(
        kernel,
        out_shape=outs,
        in_specs=specs or [VMEM] * len(args),
        out_specs=jax.tree.map(lambda _: VMEM, outs),
        scratch_shapes=scratch,
        compiler_params=pltpu.CompilerParams(vmem_limit_bytes=limit),
    )(*args)


def place_kernel(blocks, out, sem):
    row, col = lax.axis_index("row"), lax.axis_index("col")
    core = row % 2
    near = (row // 2 + core) % 2
    order = [2 * near + core, 2 * near + 1 - core, 2 * (1 - near) + 1 - core, 2 * (1 - near) + core]
    copies = []
    for m in range(4):
        for j in range(4):
            copies.append(
                pltpu.make_async_copy(blocks.at[(col + m) % 4, order[j]], out.at[m, j], sem.at[4 * m + j])
            )
    for copy in copies:
        copy.start()
    for copy in copies:
        copy.wait()


def first_kernel(plan, stored, up, down):
    slab = lax.axis_index("slab")
    up[...] = stored[plan[0, 0, slab]]
    down[...] = narrow(wide(stored[plan[0, 1, slab]]).T)


def pick_up_kernel(plan, stored, gain, out_gain, *outs):
    slab = lax.axis_index("slab")
    after = (slab + 1) % 8
    row_gain = jnp.where(after == 0, 0.0, gain[...])
    out_gain[...] = jnp.broadcast_to(row_gain, (stored.shape[2], stored.shape[1])).T
    for t, out in enumerate(outs):
        out[...] = stored[plan[t + 1, 0, after]]


def pick_down_kernel(plan, stored, *outs):
    slab = lax.axis_index("slab")
    for t, out in enumerate(outs):
        out[...] = narrow(wide(stored[plan[t + 1, 1, slab]]).T)


def stack_kernel(own, other, out):
    out[0] = own[...]
    out[1] = other[...]


def by_core_kernel(pair, moved, out):
    core = lax.axis_index("row") % 2
    out[...] = jnp.where(core == 0, pair[...], moved[...])


def up_first_kernel(blocks, x, acc):
    for m in range(4):
        acc[m] = f32dot(blocks[m, 0], x[0]) + f32dot(blocks[m, 1], x[1])


def up_last_kernel(m, blocks, x, acc, out):
    total = acc[m] + f32dot(blocks[m, 2], x[0]) + f32dot(blocks[m, 3], x[1])
    out[...] = total.astype(out.dtype)


def up_sum_kernel(own, p1, p2, p3, out):
    out[...] = narrow(own[...] + wide(p1[...]) + wide(p2[...]) + wide(p3[...]))


def up_next_kernel(own, p1, p2, p3, source, gain, out):
    carried = narrow(own[...] + wide(p1[...]) + wide(p2[...]) + wide(p3[...]))
    out[...] = narrow(wide(source[...]) + gain[...] * wide(carried))


def down_first_kernel(blocks, x0, acc):
    for j in range(4):
        acc[j] = f32dot(x0[...], blocks[0, j])


def down_last_kernel(blocks, x1, x2, x3, acc, kept, sent):
    def total(j):
        return acc[j] + f32dot(x1[...], blocks[1, j]) + f32dot(x3[...], blocks[3, j]) + f32dot(x2[...], blocks[2, j])

    sent[0] = narrow(total(2))
    sent[1] = narrow(total(3))
    kept[0] = total(0)
    kept[1] = total(1)


def down_pair_kernel(kept, got, out):
    out[...] = narrow(kept[...] + wide(got[...]))


def down_next_kernel(moved, got, source, gain, out):
    carried = narrow(wide(moved[0]) + wide(got[...]))
    out[...] = narrow(wide(source[...]) + gain[...] * wide(carried))


def down_sum_kernel(moved, got, out):
    out[...] = narrow((wide(moved[0]) + wide(got[...])).T)


def per_device(inverse, sources, coupling, plan):
    slabs, rows, cols = (lax.axis_size(a) for a in ("slab", "row", "col"))
    piece, width = sources.shape[2:]
    top = slabs - 1
    everyone = list(range(slabs))

    def swap_cores(value, active):
        pairs = [(s * rows + r, s * rows + (r ^ 1)) for s in active for r in range(rows)]
        return lax.ppermute(value, ("slab", "row"), pairs)

    def target(r):
        return r ^ 2 if r % 2 else r

    def over_slab(value, active, step):
        pairs = [(s * rows + r, ((s + step) % slabs) * rows + target(r)) for s in active for r in range(rows)]
        return lax.ppermute(value, ("slab", "row"), pairs)

    def over_half(value, active):
        pairs = [(s * rows + r, s * rows + target(r)) for s in active for r in range(rows) if r % 2]
        return lax.ppermute(value, ("slab", "row"), pairs)

    def over_col(value, active, step):
        pairs = [(s * cols + c, s * cols + (c + step) % cols) for s in active for c in range(cols)]
        return lax.ppermute(value, ("slab", "col"), pairs)

    stored = sources[0]
    plan = jnp.swapaxes(plan, 1, 2)
    down_gain = coupling[0, 1][None, :]
    piece_u = shape(piece, width)
    piece_d = shape(width, piece)
    pair_u = shape(2, piece, width)
    pair_d = shape(2, width, piece)
    kept_d = shape(2, width, piece, kind=jnp.float32)
    acc_up = shape(cols, piece, width, kind=jnp.float32)
    acc_down = shape(rows, width, piece, kind=jnp.float32)
    up_in, down_in = call(first_kernel, (piece_u, piece_d), plan, stored, specs=[SMEM, VMEM])
    shift_pairs = [(s * rows + r, ((s - 1) % slabs) * rows + r) for s in everyone for r in range(rows)]
    next_stored = lax.ppermute(stored, ("slab", "row"), shift_pairs)
    next_gain = lax.ppermute(coupling[0, 0], ("slab", "row"), shift_pairs)[None, :]
    split = inverse[0].reshape(cols, piece, rows, piece).transpose(0, 2, 1, 3)
    blocks = call(
        place_kernel, shape(cols, rows, piece, piece), split, specs=[ANY], scratch=[pltpu.SemaphoreType.DMA((16,))]
    )
    up_gain, *up_sources = call(
        pick_up_kernel,
        (shape(piece, width, kind=jnp.float32),) + (piece_u,) * (TICKS - 1),
        plan,
        next_stored,
        next_gain,
        specs=[SMEM, VMEM, VMEM],
    )
    down_sources = call(pick_down_kernel, (piece_d,) * (TICKS - 1), plan, stored, specs=[SMEM, VMEM])
    for t in range(TICKS):
        last = t == TICKS - 1
        up_on = [s for s in range(slabs) if s <= GROUPED[t]]
        down_on = [s for s in range(slabs) if s >= top - GROUPED[t]]
        senders = up_on if t == 0 else [(s - 1) % slabs for s in up_on]

        d2 = over_col(down_in, down_on, -2)
        d1 = over_col(down_in, down_on, -1)
        d3 = over_col(down_in, down_on, -3)
        other = swap_cores(up_in, senders)
        acc_d = call(down_first_kernel, acc_down, blocks, down_in)
        pair = call(stack_kernel, pair_u, up_in, other)
        if t == 0:
            moved = over_half(pair, up_on)
            moved = call(by_core_kernel, pair_u, pair, moved)
        else:
            moved = over_slab(pair, senders, 1)
        kept, sent = call(down_last_kernel, (kept_d, pair_d), blocks, d1, d2, d3, acc_d)
        got = swap_cores(sent, down_on)
        other = swap_cores(moved, up_on)
        acc_u = call(up_first_kernel, acc_up, blocks, moved)
        pair = call(down_pair_kernel, pair_d, kept, got)
        if last:
            moved_d = over_half(pair, down_on)
            moved_d = call(by_core_kernel, pair_d, pair, moved_d)
            receivers = down_on
        else:
            receivers = [s - 1 for s in down_on if s > 0]
            moved_d = over_slab(pair, [s for s in down_on if s > 0], -1)
        parts = {}
        for m in (2, 1, 3, 0):
            kind = shape(piece, width, kind=jnp.bfloat16 if m else jnp.float32)
            parts[m] = call(lambda *refs, m=m: up_last_kernel(m, *refs), kind, blocks, other, acc_u)
            if m:
                parts[m] = over_col(parts[m], up_on, m)
        got = swap_cores(moved_d[1], receivers)
        if last:
            up_out = call(up_sum_kernel, piece_u, parts[0], parts[1], parts[2], parts[3])
            down_out = call(down_sum_kernel, piece_u, moved_d, got)
        else:
            down_in = call(down_next_kernel, piece_d, moved_d, got, down_sources[t], down_gain)
            up_in = call(up_next_kernel, piece_u, parts[0], parts[1], parts[2], parts[3], up_sources[t], up_gain)
    return (up_out[None], down_out[None])


def solution(mesh):
    placed = (
        P("slab", "row", None, "col"),
        P("slab", None, ("row", "col"), None),
        P("slab", None, ("row", "col")),
        P(),
    )
    return jax.shard_map(
        per_device,
        mesh=mesh,
        in_specs=placed,
        out_specs=(P("slab", ("row", "col"), None), P("slab", ("row", "col"), None)),
        check_vma=False,
    )
```

```python
import jax
import jax.numpy as jnp
from jax import lax
from jax.experimental import pallas as pl
from jax.experimental.pallas import tpu as pltpu
from jax.sharding import PartitionSpec as P

TICKS = 6
GROUPED = (7, 7, 7, 7, 7, 7)

VMEM = pl.BlockSpec(memory_space=pltpu.VMEM)
SMEM = pl.BlockSpec(memory_space=pltpu.SMEM)
ANY = pl.BlockSpec(memory_space=pl.ANY)


def f32dot(a, b):
    return jnp.dot(a, b, preferred_element_type=jnp.float32)


def wide(value):
    return value.astype(jnp.float32)


def narrow(value):
    return value.astype(jnp.bfloat16)


def shape(*lengths, kind=jnp.bfloat16):
    return jax.ShapeDtypeStruct(lengths, kind)


def call(kernel, outs, *args, specs=None, scratch=(), limit=24 << 20):
    return pl.pallas_call(
        kernel,
        out_shape=outs,
        in_specs=specs or [VMEM] * len(args),
        out_specs=jax.tree.map(lambda _: VMEM, outs),
        scratch_shapes=scratch,
        compiler_params=pltpu.CompilerParams(vmem_limit_bytes=limit),
    )(*args)


def place_kernel(source, out):
    row, col = lax.axis_index("row"), lax.axis_index("col")
    core = row % 2
    near = (row // 2 + core) % 2
    chunk = 256
    per_piece = out.shape[2] // chunk

    def step(i, carry):
        turned = jnp.swapaxes(source[pl.ds(i * chunk, chunk)], 0, 1)
        m = (i // per_piece - col + 4) % 4
        for k in range(4):
            same = (core + k) % 2
            j = jnp.where(k // 2 == near, same, 3 - same)
            out[m, j, pl.ds((i % per_piece) * chunk, chunk), :] = turned[k]
        return carry

    lax.fori_loop(0, 4 * per_piece, step, 0)


def first_kernel(plan, stored, up, down, after):
    slab = lax.axis_index("slab")
    up[...] = stored[plan[0, 0, slab]]
    after[...] = stored[plan[1, 0, slab]]
    down[...] = narrow(wide(stored[plan[0, 1, slab]]).T)


def spread_kernel(gain, out):
    after = (lax.axis_index("slab") + 1) % 8
    row_gain = jnp.where(after == 0, 0.0, gain[...])
    out[...] = jnp.broadcast_to(row_gain, (out.shape[1], out.shape[0])).T


def pick_up_kernel(plan, stored, *outs):
    slab = lax.axis_index("slab")
    for n, out in enumerate(outs):
        for t in range(2):
            out[t] = stored[plan[2 + 2 * n + t, 0, slab]]


def pick_down_kernel(plan, stored, out):
    slab = lax.axis_index("slab")

    def step(t, carry):
        out[t] = narrow(wide(stored[plan[t + 1, 1, slab]]).T)
        return carry

    lax.fori_loop(0, TICKS - 1, step, 0)


def stack_kernel(own, other, out):
    out[0] = own[...]
    out[1] = other[...]


def up_first_kernel(blocks, x, acc):
    def step(m, carry):
        acc[m] = f32dot(blocks[m, 0], x[0]) + f32dot(blocks[m, 1], x[1])
        return carry

    lax.fori_loop(0, 4, step, 0, unroll=2)


def up_last_kernel(ms, blocks, x, acc, *outs):
    for m, out in zip(ms, outs):
        total = acc[m] + f32dot(blocks[m, 2], x[0]) + f32dot(blocks[m, 3], x[1])
        out[...] = total.astype(out.dtype)


def up_sum_kernel(own, p1, p2, p3, out):
    out[...] = narrow(own[...] + wide(p1[...]) + wide(p2[...]) + wide(p3[...]))


def up_next_kernel(t, own, p1, p2, p3, source, gain, out):
    carried = narrow(own[...] + wide(p1[...]) + wide(p2[...]) + wide(p3[...]))
    chosen = source[...] if t == 0 else source[(t - 1) % 2]
    out[...] = narrow(wide(chosen) + gain[...] * wide(carried))


def down_first_kernel(blocks, x0, acc):
    def step(j, carry):
        acc[j] = f32dot(x0[...], blocks[0, j])
        return carry

    lax.fori_loop(0, 4, step, 0, unroll=2)


def down_last_kernel(blocks, x1, x2, x3, acc, kept, sent):
    def total(j):
        return acc[j] + f32dot(x1[...], blocks[1, j]) + f32dot(x3[...], blocks[3, j]) + f32dot(x2[...], blocks[2, j])

    def step(j, carry):
        sent[j] = narrow(total(2 + j))
        kept[j] = total(j)
        return carry

    lax.fori_loop(0, 2, step, 0)


def down_pair_kernel(kept, got, out):
    out[...] = narrow(kept[...] + wide(got[...]))


def down_next_kernel(t, moved, got, source, gain, out):
    carried = narrow(wide(moved[0]) + wide(got[...]))
    out[...] = narrow(wide(source[t]) + gain[...] * wide(carried))


def down_sum_kernel(moved, got, out):
    out[...] = narrow((wide(moved[0]) + wide(got[...])).T)


def per_device(inverse, sources, coupling, plan):
    slabs, rows, cols = (lax.axis_size(a) for a in ("slab", "row", "col"))
    piece, width = sources.shape[2:]
    top = slabs - 1
    everyone = list(range(slabs))

    def swap_cores(value, active):
        pairs = [(s * rows + r, s * rows + (r ^ 1)) for s in active for r in range(rows)]
        return lax.ppermute(value, ("slab", "row"), pairs)

    def target(r):
        return r ^ 2 if r % 2 else r

    def over_slab(value, active, step):
        pairs = [(s * rows + r, ((s + step) % slabs) * rows + target(r)) for s in active for r in range(rows)]
        return lax.ppermute(value, ("slab", "row"), pairs)

    def over_half(value, active):
        pairs = [(s * rows + r, s * rows + target(r)) for s in active for r in range(rows)]
        return lax.ppermute(value, ("slab", "row"), pairs)

    def over_col(value, active, step):
        pairs = [(s * cols + c, s * cols + (c + step) % cols) for s in active for c in range(cols)]
        return lax.ppermute(value, ("slab", "col"), pairs)

    stored = sources[0]
    plan = jnp.swapaxes(plan, 1, 2)
    down_gain = jnp.where(lax.axis_index("slab") == top, 0.0, coupling[0, 1][None, :])
    piece_u = shape(piece, width)
    piece_d = shape(width, piece)
    pair_u = shape(2, piece, width)
    pair_d = shape(2, width, piece)
    kept_d = shape(2, width, piece, kind=jnp.float32)
    acc_up = shape(cols, piece, width, kind=jnp.float32)
    acc_down = shape(rows, width, piece, kind=jnp.float32)
    up_in, down_in, after = call(first_kernel, (piece_u, piece_d, piece_u), plan, stored, specs=[SMEM, VMEM])
    shift_pairs = [(s * rows + r, ((s - 1) % slabs) * rows + r) for s in everyone for r in range(rows)]
    next_source = lax.ppermute(after, ("slab", "row"), shift_pairs)
    later = call(pick_up_kernel, (pair_u, pair_u), plan, stored, specs=[SMEM, VMEM])
    later = [lax.ppermute(value, ("slab", "row"), shift_pairs) for value in later]
    next_gain = lax.ppermute(coupling[0, 0], ("slab", "row"), shift_pairs)[None, :]
    blocks = call(place_kernel, shape(cols, rows, piece, piece), inverse[0], limit=40 << 20)
    up_gain = call(spread_kernel, shape(piece, width, kind=jnp.float32), next_gain)
    down_sources = call(pick_down_kernel, shape(TICKS - 1, width, piece), plan, stored, specs=[SMEM, VMEM])
    for t in range(TICKS):
        last = t == TICKS - 1
        up_on = [s for s in range(slabs) if s <= GROUPED[t]]
        down_on = [s for s in range(slabs) if s >= top - GROUPED[t]]
        senders = up_on if t == 0 else [(s - 1) % slabs for s in up_on]

        d2 = over_col(down_in, down_on, -2)
        d1 = over_col(down_in, down_on, -1)
        d3 = over_col(down_in, down_on, -3)
        other = swap_cores(up_in, senders)
        acc_d = call(down_first_kernel, acc_down, blocks, down_in)
        pair = call(stack_kernel, pair_u, up_in, other)
        if t == 0:
            moved = over_half(pair, up_on)
        else:
            moved = over_slab(pair, senders, 1)
        kept, sent = call(down_last_kernel, (kept_d, pair_d), blocks, d1, d2, d3, acc_d)
        got = swap_cores(sent, down_on)
        other = swap_cores(moved, up_on)
        acc_u = call(up_first_kernel, acc_up, blocks, moved)
        pair = call(down_pair_kernel, pair_d, kept, got)
        if last:
            moved_d = over_half(pair, down_on)
        else:
            moved_d = over_slab(pair, down_on, -1)
        parts = {}
        for ms in ((2,), (1, 3), (0,)):
            kinds = tuple(shape(piece, width, kind=jnp.bfloat16 if m else jnp.float32) for m in ms)
            made = call(lambda *refs, ms=ms: up_last_kernel(ms, *refs), kinds, blocks, other, acc_u)
            for m, part in zip(ms, made):
                parts[m] = over_col(part, up_on, m) if m else part
        got = swap_cores(moved_d[1], down_on)
        if last:
            up_out = call(up_sum_kernel, piece_u, parts[0], parts[1], parts[2], parts[3])
            down_out = call(down_sum_kernel, piece_u, moved_d, got)
        else:
            down_in = call(
                lambda *refs, t=t: down_next_kernel(t, *refs), piece_d, moved_d, got, down_sources, down_gain
            )
            up_in = call(
                lambda *refs, t=t: up_next_kernel(t, *refs),
                piece_u,
                parts[0],
                parts[1],
                parts[2],
                parts[3],
                later[(t - 1) // 2] if t else next_source,
                up_gain,
            )
    return (up_out[None], down_out[None])


def solution(mesh):
    placed = (
        P("slab", "row", None, "col"),
        P("slab", None, ("row", "col"), None),
        P("slab", None, ("row", "col")),
        P(),
    )
    return jax.shard_map(
        per_device,
        mesh=mesh,
        in_specs=placed,
        out_specs=(P("slab", ("row", "col"), None), P("slab", ("row", "col"), None)),
        check_vma=False,
    )
```

```python
import jax
import jax.numpy as jnp
from jax import lax
from jax.experimental import pallas as pl
from jax.experimental.pallas import tpu as pltpu
from jax.sharding import PartitionSpec as P

TICKS = 6
GROUPED = (7, 7, 7, 7, 7, 7)

VMEM = pl.BlockSpec(memory_space=pltpu.VMEM)
SMEM = pl.BlockSpec(memory_space=pltpu.SMEM)
HBM = pl.BlockSpec(memory_space=pltpu.HBM)


def f32dot(a, b):
    return jnp.dot(a, b, preferred_element_type=jnp.float32)


def wide(value):
    return value.astype(jnp.float32)


def narrow(value):
    return value.astype(jnp.bfloat16)


def shape(*lengths, kind=jnp.bfloat16):
    return jax.ShapeDtypeStruct(lengths, kind)


def call(kernel, outs, *args, specs=None, scratch=(), limit=24 << 20):
    return pl.pallas_call(
        kernel,
        out_shape=outs,
        in_specs=specs or [VMEM] * len(args),
        out_specs=jax.tree.map(lambda _: VMEM, outs),
        scratch_shapes=scratch,
        compiler_params=pltpu.CompilerParams(vmem_limit_bytes=limit),
    )(*args)


def place_kernel(source, out, buffer, sem):
    row, col = lax.axis_index("row"), lax.axis_index("col")
    core = row % 2
    near = (row // 2 + core) % 2
    chunk = buffer.shape[1]
    count = buffer.shape[0]
    per_piece = out.shape[2] // chunk

    def copy(i):
        return pltpu.make_async_copy(source.at[pl.ds(i * chunk, chunk)], buffer.at[i], sem.at[i])

    for i in range(count):
        copy(i).start()

    def step(i, carry):
        copy(i).wait()
        turned = jnp.swapaxes(buffer[i], 0, 1)
        m = (i // per_piece - col + 4) % 4
        for k in range(4):
            same = (core + k) % 2
            j = jnp.where(k // 2 == near, same, 3 - same)
            out[m, j, pl.ds((i % per_piece) * chunk, chunk), :] = turned[k]
        return carry

    lax.fori_loop(0, count, step, 0)


def first_kernel(plan, stored, up, down, after):
    slab = lax.axis_index("slab")
    up[...] = stored[plan[0, 0, slab]]
    down[...] = narrow(wide(stored[plan[0, 1, slab]]).T)
    after[0] = stored[plan[1, 0, slab]]
    after[1] = stored[plan[2, 0, slab]]


def spread_kernel(gain, out):
    row_gain = jnp.where(lax.axis_index("slab") == 7, 0.0, gain[...])
    out[...] = jnp.broadcast_to(row_gain, (out.shape[1], out.shape[0])).T


def pick_up_kernel(plan, stored, out):
    slab = lax.axis_index("slab")
    for t in range(3, TICKS):
        out[t - 3] = stored[plan[t, 0, slab]]


def pick_down_kernel(plan, stored, out):
    slab = lax.axis_index("slab")

    def step(t, carry):
        out[t] = narrow(wide(stored[plan[t + 1, 1, slab]]).T)
        return carry

    lax.fori_loop(0, TICKS - 1, step, 0)


def stack_kernel(own, other, out):
    out[0] = own[...]
    out[1] = other[...]


def up_first_kernel(blocks, x, acc):
    def step(m, carry):
        acc[m] = f32dot(blocks[m, 0], x[0]) + f32dot(blocks[m, 1], x[1])
        return carry

    lax.fori_loop(0, 4, step, 0, unroll=2)


def up_last_kernel(blocks, x, acc, out):
    def step(m, carry):
        out[m] = narrow(acc[m] + f32dot(blocks[m, 2], x[0]) + f32dot(blocks[m, 3], x[1]))
        return carry

    lax.fori_loop(0, 4, step, 0)


def up_sum_kernel(own, p1, p2, p3, out):
    out[...] = narrow(wide(own[0]) + wide(p1[...]) + wide(p2[...]) + wide(p3[...]))


def up_next_kernel(t, own, p1, p2, p3, source, gain, out):
    carried = narrow(wide(own[0]) + wide(p1[...]) + wide(p2[...]) + wide(p3[...]))
    chosen = source[t if t < 2 else t - 2]
    out[...] = narrow(wide(chosen) + gain[...] * wide(carried))


def down_first_kernel(blocks, x0, acc):
    def step(j, carry):
        acc[j] = f32dot(x0[...], blocks[0, j])
        return carry

    lax.fori_loop(0, 4, step, 0)


def down_more_kernel(blocks, x1, x2, acc, out):
    def step(j, carry):
        out[j] = acc[j] + f32dot(x1[...], blocks[1, j]) + f32dot(x2[...], blocks[2, j])
        return carry

    lax.fori_loop(0, 4, step, 0, unroll=2)


def down_last_kernel(blocks, x3, acc, kept, sent):
    def step(j, carry):
        sent[j] = narrow(acc[2 + j] + f32dot(x3[...], blocks[3, 2 + j]))
        kept[j] = acc[j] + f32dot(x3[...], blocks[3, j])
        return carry

    lax.fori_loop(0, 2, step, 0)


def down_pair_kernel(kept, got, out):
    out[...] = narrow(kept[...] + wide(got[...]))


def down_next_kernel(t, moved, got, source, gain, out):
    carried = narrow(wide(moved[0]) + wide(got[...]))
    used = jnp.where(lax.axis_index("slab") == 7, 0.0, gain[...])
    out[...] = narrow(wide(source[t]) + used * wide(carried))


def down_sum_kernel(moved, got, out):
    out[...] = narrow((wide(moved[0]) + wide(got[...])).T)


def per_device(inverse, sources, coupling, plan):
    slabs, rows, cols = (lax.axis_size(a) for a in ("slab", "row", "col"))
    piece, width = sources.shape[2:]
    top = slabs - 1
    everyone = list(range(slabs))

    def swap_cores(value, active):
        pairs = [(s * rows + r, s * rows + (r ^ 1)) for s in active for r in range(rows)]
        return lax.ppermute(value, ("slab", "row"), pairs)

    def target(r):
        return r ^ 2 if r % 2 else r

    def over_slab(value, active, step):
        pairs = [(s * rows + r, ((s + step) % slabs) * rows + target(r)) for s in active for r in range(rows)]
        return lax.ppermute(value, ("slab", "row"), pairs)

    def over_half(value, active):
        pairs = [(s * rows + r, s * rows + target(r)) for s in active for r in range(rows)]
        return lax.ppermute(value, ("slab", "row"), pairs)

    def over_col(value, active, step):
        pairs = [(s * cols + c, s * cols + (c + step) % cols) for s in active for c in range(cols)]
        return lax.ppermute(value, ("slab", "col"), pairs)

    stored = sources[0]
    plan = jnp.swapaxes(plan, 1, 2)
    down_gain = coupling[0, 1][None, :]
    piece_u = shape(piece, width)
    piece_d = shape(width, piece)
    pair_u = shape(2, piece, width)
    pair_d = shape(2, width, piece)
    kept_d = shape(2, width, piece, kind=jnp.float32)
    acc_up = shape(cols, piece, width, kind=jnp.float32)
    acc_down = shape(rows, width, piece, kind=jnp.float32)
    up_in, down_in, after = call(first_kernel, (piece_u, piece_d, pair_u), plan, stored, specs=[SMEM, VMEM])
    shift_pairs = [(s * rows + r, ((s - 1) % slabs) * rows + r) for s in everyone for r in range(rows)]
    next_source = lax.ppermute(after, ("slab", "row"), shift_pairs)
    later = call(pick_up_kernel, shape(TICKS - 3, piece, width), plan, stored, specs=[SMEM, VMEM])
    later = lax.ppermute(later, ("slab", "row"), shift_pairs)
    next_gain = lax.ppermute(coupling[0, 0], ("slab", "row"), shift_pairs)[None, :]
    blocks = call(
        place_kernel,
        shape(cols, rows, piece, piece),
        inverse[0],
        specs=[HBM],
        scratch=[pltpu.VMEM((8, 256, rows, piece), jnp.bfloat16), pltpu.SemaphoreType.DMA((8,))],
        limit=40 << 20,
    )
    up_gain = call(spread_kernel, shape(piece, width, kind=jnp.float32), next_gain)
    down_sources = call(pick_down_kernel, shape(TICKS - 1, width, piece), plan, stored, specs=[SMEM, VMEM])
    for t in range(TICKS):
        last = t == TICKS - 1
        up_on = [s for s in range(slabs) if s <= GROUPED[t]]
        down_on = [s for s in range(slabs) if s >= top - GROUPED[t]]
        senders = up_on if t == 0 else [(s - 1) % slabs for s in up_on]

        d2 = over_col(down_in, down_on, -2)
        d1 = over_col(down_in, down_on, -1)
        d3 = over_col(down_in, down_on, -3)
        other = swap_cores(up_in, senders)
        acc_d = call(down_first_kernel, acc_down, blocks, down_in)
        pair = call(stack_kernel, pair_u, up_in, other)
        if t == 0:
            moved = over_half(pair, up_on)
        else:
            moved = over_slab(pair, senders, 1)
        acc_d = call(down_more_kernel, acc_down, blocks, d1, d2, acc_d)
        kept, sent = call(down_last_kernel, (kept_d, pair_d), blocks, d3, acc_d)
        got = swap_cores(sent, down_on)
        other = swap_cores(moved, up_on)
        acc_u = call(up_first_kernel, acc_up, blocks, moved)
        pair = call(down_pair_kernel, pair_d, kept, got)
        if last:
            moved_d = over_half(pair, down_on)
        else:
            moved_d = over_slab(pair, down_on, -1)
        made = call(up_last_kernel, shape(cols, piece, width), blocks, other, acc_u)
        parts = [made] + [over_col(made[m], up_on, m) for m in (1, 2, 3)]
        got = swap_cores(moved_d[1], down_on)
        if last:
            up_out = call(up_sum_kernel, piece_u, parts[0], parts[1], parts[2], parts[3])
            down_out = call(down_sum_kernel, piece_u, moved_d, got)
        else:
            down_in = call(
                lambda *refs, t=t: down_next_kernel(t, *refs), piece_d, moved_d, got, down_sources, down_gain
            )
            up_in = call(
                lambda *refs, t=t: up_next_kernel(t, *refs),
                piece_u,
                parts[0],
                parts[1],
                parts[2],
                parts[3],
                later if t > 1 else next_source,
                up_gain,
            )
    return (up_out[None], down_out[None])


def solution(mesh):
    placed = (
        P("slab", "row", None, "col"),
        P("slab", None, ("row", "col"), None),
        P("slab", None, ("row", "col")),
        P(),
    )
    return jax.shard_map(
        per_device,
        mesh=mesh,
        in_specs=placed,
        out_specs=(P("slab", ("row", "col"), None), P("slab", ("row", "col"), None)),
        check_vma=False,
    )
```

```python
import jax
import jax.numpy as jnp
from jax import lax
from jax.experimental import pallas as pl
from jax.experimental.pallas import tpu as pltpu
from jax.sharding import PartitionSpec as P

TICKS = 6
GROUPED = (7, 7, 7, 7, 7, 7)

VMEM = pl.BlockSpec(memory_space=pltpu.VMEM)
SMEM = pl.BlockSpec(memory_space=pltpu.SMEM)
HBM = pl.BlockSpec(memory_space=pltpu.HBM)


def f32dot(a, b):
    return jnp.dot(a, b, preferred_element_type=jnp.float32)


def wide(value):
    return value.astype(jnp.float32)


def narrow(value):
    return value.astype(jnp.bfloat16)


def shape(*lengths, kind=jnp.bfloat16):
    return jax.ShapeDtypeStruct(lengths, kind)


def call(kernel, outs, *args, specs=None, scratch=(), limit=24 << 20):
    return pl.pallas_call(
        kernel,
        out_shape=outs,
        in_specs=specs or [VMEM] * len(args),
        out_specs=jax.tree.map(lambda _: VMEM, outs),
        scratch_shapes=scratch,
        compiler_params=pltpu.CompilerParams(vmem_limit_bytes=limit),
    )(*args)


def place_kernel(source, out, buffer, sem):
    row, col = lax.axis_index("row"), lax.axis_index("col")
    core = row % 2
    near = (row // 2 + core) % 2
    chunk = buffer.shape[1]
    count = buffer.shape[0]
    per_piece = out.shape[2] // chunk

    def copy(i):
        return pltpu.make_async_copy(source.at[pl.ds(i * chunk, chunk)], buffer.at[i], sem.at[i])

    for i in range(count):
        copy(i).start()

    def step(i, carry):
        copy(i).wait()
        turned = jnp.swapaxes(buffer[i], 0, 1)
        m = (i // per_piece - col + 4) % 4
        for k in range(4):
            same = (core + k) % 2
            j = jnp.where(k // 2 == near, same, 3 - same)
            out[m, j, pl.ds((i % per_piece) * chunk, chunk), :] = turned[k]
        return carry

    lax.fori_loop(0, count, step, 0)


def turn_kernel(blocks, out):
    def step(i, carry):
        out[i // 4, i % 4] = blocks[i // 4, i % 4].T
        return carry

    lax.fori_loop(0, 16, step, 0)


def turned(value):
    return narrow(wide(value).T)


def first_kernel(plan, stored, up, down):
    slab = lax.axis_index("slab")
    down[...] = turned(stored[plan[0, 1, slab]])
    up[...] = turned(stored[plan[0, 0, slab]])


def pick_up_kernel(plan, stored, out):
    slab = lax.axis_index("slab")

    def step(t, carry):
        out[t] = turned(stored[plan[t + 3, 0, slab]])
        return carry

    lax.fori_loop(0, TICKS - 3, step, 0)


def pick_near_kernel(plan, stored, out):
    slab = lax.axis_index("slab")

    def step(t, carry):
        out[t] = turned(stored[plan[t + 1, 0, slab]])
        return carry

    lax.fori_loop(0, 2, step, 0)


def pick_down_kernel(plan, stored, out):
    slab = lax.axis_index("slab")

    def step(t, carry):
        out[t] = turned(stored[plan[t + 1, 1, slab]])
        return carry

    lax.fori_loop(0, TICKS - 1, step, 0)


def stack_kernel(own, other, out):
    out[0] = own[...]
    out[1] = other[...]


def up_first_kernel(blocks, x, acc):
    def step(m, carry):
        acc[m] = f32dot(x[0], blocks[m, 0]) + f32dot(x[1], blocks[m, 1])
        return carry

    lax.fori_loop(0, 4, step, 0, unroll=2)


def up_last_kernel(blocks, x, acc, out):
    def step(m, carry):
        out[m] = narrow(acc[m] + f32dot(x[0], blocks[m, 2]) + f32dot(x[1], blocks[m, 3]))
        return carry

    lax.fori_loop(0, 4, step, 0, unroll=True)


def up_sum_kernel(own, p1, p2, p3, out):
    out[...] = narrow((wide(own[0]) + wide(p1[...]) + wide(p2[...]) + wide(p3[...])).T)


def up_next_kernel(t, own, p1, p2, p3, source, gain, out):
    carried = narrow(wide(own[0]) + wide(p1[...]) + wide(p2[...]) + wide(p3[...]))
    chosen = source[t if t < 2 else t - 2]
    used = jnp.where(lax.axis_index("slab") == 7, 0.0, gain[...])
    out[...] = narrow(wide(chosen) + used * wide(carried))


def down_first_kernel(blocks, x0, acc):
    def step(j, carry):
        acc[j] = f32dot(x0[...], blocks[0, j])
        return carry

    lax.fori_loop(0, 4, step, 0)


def down_more_kernel(blocks, x1, x2, acc, out):
    def step(j, carry):
        out[j] = acc[j] + f32dot(x1[...], blocks[1, j]) + f32dot(x2[...], blocks[2, j])
        return carry

    lax.fori_loop(0, 4, step, 0, unroll=2)


def down_last_kernel(blocks, x3, acc, kept, sent):
    def step(j, carry):
        sent[j] = narrow(acc[2 + j] + f32dot(x3[...], blocks[3, 2 + j]))
        kept[j] = acc[j] + f32dot(x3[...], blocks[3, j])
        return carry

    lax.fori_loop(0, 2, step, 0, unroll=True)


def down_pair_kernel(kept, got, out):
    out[...] = narrow(kept[...] + wide(got[...]))


def down_next_kernel(t, moved, got, source, gain, out):
    carried = narrow(wide(moved[0]) + wide(got[...]))
    used = jnp.where(lax.axis_index("slab") == 7, 0.0, gain[...])
    out[...] = narrow(wide(source[t]) + used * wide(carried))


def down_sum_kernel(moved, got, out):
    out[...] = narrow((wide(moved[0]) + wide(got[...])).T)


def per_device(inverse, sources, coupling, plan):
    slabs, rows, cols = (lax.axis_size(a) for a in ("slab", "row", "col"))
    piece, width = sources.shape[2:]
    top = slabs - 1
    everyone = list(range(slabs))

    def swap_cores(value, active):
        pairs = [(s * rows + r, s * rows + (r ^ 1)) for s in active for r in range(rows)]
        return lax.ppermute(value, ("slab", "row"), pairs)

    def target(r):
        return r ^ 2 if r % 2 else r

    def over_slab(value, active, step):
        pairs = [(s * rows + r, ((s + step) % slabs) * rows + target(r)) for s in active for r in range(rows)]
        return lax.ppermute(value, ("slab", "row"), pairs)

    def over_half(value, active):
        pairs = [(s * rows + r, s * rows + target(r)) for s in active for r in range(rows)]
        return lax.ppermute(value, ("slab", "row"), pairs)

    def over_col(value, active, step):
        pairs = [(s * cols + c, s * cols + (c + step) % cols) for s in active for c in range(cols)]
        return lax.ppermute(value, ("slab", "col"), pairs)

    stored = sources[0]
    plan = jnp.swapaxes(plan, 1, 2)
    down_gain = coupling[0, 1][None, :]
    piece_u = shape(piece, width)
    piece_d = shape(width, piece)
    pair_d = shape(2, width, piece)
    kept_d = shape(2, width, piece, kind=jnp.float32)
    acc_up = shape(cols, width, piece, kind=jnp.float32)
    acc_down = shape(rows, width, piece, kind=jnp.float32)
    up_in, down_in = call(first_kernel, (piece_d, piece_d), plan, stored, specs=[SMEM, VMEM])
    shift_pairs = [(s * rows + r, ((s - 1) % slabs) * rows + r) for s in everyone for r in range(rows)]
    near = call(pick_near_kernel, pair_d, plan, stored, specs=[SMEM, VMEM])
    next_source = lax.ppermute(near, ("slab", "row"), shift_pairs)
    later = call(pick_up_kernel, shape(TICKS - 3, width, piece), plan, stored, specs=[SMEM, VMEM])
    later = lax.ppermute(later, ("slab", "row"), shift_pairs)
    next_gain = lax.ppermute(coupling[0, 0], ("slab", "row"), shift_pairs)[None, :]
    blocks = call(
        place_kernel,
        shape(cols, rows, piece, piece),
        inverse[0],
        specs=[HBM],
        scratch=[pltpu.VMEM((8, 256, rows, piece), jnp.bfloat16), pltpu.SemaphoreType.DMA((8,))],
        limit=40 << 20,
    )
    columns = call(turn_kernel, shape(cols, rows, piece, piece), blocks, limit=20 << 20)
    down_sources = call(pick_down_kernel, shape(TICKS - 1, width, piece), plan, stored, specs=[SMEM, VMEM])
    for t in range(TICKS):
        last = t == TICKS - 1
        up_on = [s for s in range(slabs) if s <= GROUPED[t]]
        down_on = [s for s in range(slabs) if s >= top - GROUPED[t]]
        senders = up_on if t == 0 else [(s - 1) % slabs for s in up_on]

        d2 = over_col(down_in, down_on, -2)
        d1 = over_col(down_in, down_on, -1)
        d3 = over_col(down_in, down_on, -3)
        other = swap_cores(up_in, senders)
        acc_d = call(down_first_kernel, acc_down, blocks, down_in)
        pair = call(stack_kernel, pair_d, up_in, other)
        if t == 0:
            moved = over_half(pair, up_on)
        else:
            moved = over_slab(pair, senders, 1)
        acc_d = call(down_more_kernel, acc_down, blocks, d1, d2, acc_d)
        kept, sent = call(down_last_kernel, (kept_d, pair_d), blocks, d3, acc_d)
        got = swap_cores(sent, down_on)
        other = swap_cores(moved, up_on)
        acc_u = call(up_first_kernel, acc_up, columns, moved)
        pair = call(down_pair_kernel, pair_d, kept, got)
        if last:
            moved_d = over_half(pair, down_on)
        else:
            moved_d = over_slab(pair, down_on, -1)
        made = call(up_last_kernel, shape(cols, width, piece), columns, other, acc_u)
        parts = [made] + [over_col(made[m], up_on, m) for m in (1, 2, 3)]
        got = swap_cores(moved_d[1], down_on)
        if last:
            up_out = call(up_sum_kernel, piece_u, parts[0], parts[1], parts[2], parts[3])
            down_out = call(down_sum_kernel, piece_u, moved_d, got)
        else:
            down_in = call(
                lambda *refs, t=t: down_next_kernel(t, *refs), piece_d, moved_d, got, down_sources, down_gain
            )
            up_in = call(
                lambda *refs, t=t: up_next_kernel(t, *refs),
                piece_d,
                parts[0],
                parts[1],
                parts[2],
                parts[3],
                later if t > 1 else next_source,
                next_gain,
            )
    return (up_out[None], down_out[None])


def solution(mesh):
    placed = (
        P("slab", "row", None, "col"),
        P("slab", None, ("row", "col"), None),
        P("slab", None, ("row", "col")),
        P(),
    )
    return jax.shard_map(
        per_device,
        mesh=mesh,
        in_specs=placed,
        out_specs=(P("slab", ("row", "col"), None), P("slab", ("row", "col"), None)),
        check_vma=False,
    )
```
